128 devices in a mesh: seq: 32 (over y, x, core), chan: 4 (over z).
Axes of the slice: x: 4, y: 4, z: 4, core: 2. Of those that a mesh axis runs over, the one named last changes fastest.
Arguments:
- doc_ids: int32 [8192], replicated, may hold values from 0 to 15, never falling along the last dimension, each value on 1 to 1024 neighbouring positions
- attn_queries: bfloat16 [8192, 8192], P(('seq', 'chan')), may hold values from -6 to 6
- attn_keys: bfloat16 [8192, 8192], P(('seq', 'chan')), may hold values from -6 to 6
- attn_values: bfloat16 [8192, 8192], P(('seq', 'chan')), may hold values from -6 to 6
- attn_cot: bfloat16 [8192, 8192], P(('seq', 'chan')), may hold values from -6 to 6
Outputs:
- attn_out: bfloat16 [8192, 8192], P('seq', 'chan')
- query_grad: bfloat16 [8192, 8192], P('seq', 'chan')
- key_grad: bfloat16 [8192, 8192], P('seq', 'chan')
- value_grad: bfloat16 [8192, 8192], P('seq', 'chan')
The draws below stay inside these ranges and needn't reach their ends.
Inputs may be any that keep to these rules, and one draw needn't show every extreme that they name: `doc_ids`: documents are runs of equal ids that never fall; each holds 1 to 1024 tokens and one holds exactly 1024.
All inputs are finite; a program needn't handle non-finite values.
Results may differ from the reference program's by a relative error of at most 0.03.
Values may be sent and summed in bfloat16 or wider, within the bound.
A program may use at most 256 MiB of HBM per device.

```python
import math
import jax
import jax.numpy as jnp
import numpy as np
from jax import lax

HEAD_DIM = 128
HEADS = 64
TOK_DEV = 256
SPAN_SH = 4
DOC_MAX = 1024
TOKENS = 8192
DOCS = 16


def drawn_pair(key):
    first_key = jax.random.fold_in(key, 17)
    second_key = jax.random.fold_in(key, 29)
    total_width = HEADS * HEAD_DIM
    query_part = jnp.clip(jax.random.normal(first_key, (TOKENS, total_width), jnp.float32), -6.0, 6.0)
    key_part = jnp.clip(jax.random.normal(second_key, (TOKENS, total_width), jnp.float32), -6.0, 6.0)
    return (query_part, key_part)


def draw_attn_queries(key, part):
    return drawn_pair(key)[0].astype(jnp.bfloat16)


def draw_attn_keys(key, part):
    return drawn_pair(key)[1].astype(jnp.bfloat16)


def steps_of(rng, shape, cuts, smallest, high):
    gain, own = 1.0, jax.random.fold_in(rng, 6)
    for position, shards_of in cuts:
        heights = jnp.exp(jax.random.uniform(jax.random.fold_in(own, position), (shards_of,), jnp.float32, smallest / len(cuts), high / len(cuts)))
        gain = gain * jnp.repeat(heights, shape[position] // shards_of).reshape([-1 if axis == position else 1 for axis in range(len(shape))])
    return gain


def split_up(count, total, most, slope):
    loads = [(1 << 20) // math.isqrt(rank ** slope) + 1 for rank in range(2, count + 1)]
    spare, given = total - most - (count - 1), [1] * (count - 1)
    while spare > 0:
        free = [i for i in range(count - 1) if given[i] < most]
        whole, remaining = sum([loads[i] for i in free]), spare
        for i in free:
            extra = min(most - given[i], max(1, remaining * loads[i] // whole), spare)
            given[i] = given[i] + extra
            spare = spare - extra
    return np.array([most] + given)


def ragged(key, count, total, bound, slope):
    if count == 2:
        one = jax.random.randint(key, (), max(1, total - bound), min(bound, total - 1) + 1)
        return jnp.stack([one, total - one])
    sizes = jnp.asarray(split_up(count, total, bound, slope), jnp.int32)
    pairs = (count - 1) // 2
    donor, sink = sizes[1:1 + 2 * pairs:2], sizes[2:2 + 2 * pairs:2]
    slack = jnp.minimum(donor - 1, bound - sink)
    shifted = jax.random.randint(jax.random.fold_in(key, 1), (pairs,), 0, 1 << 20) % (slack + 1)
    sizes = sizes.at[1:1 + 2 * pairs:2].set(donor - shifted).at[2:2 + 2 * pairs:2].set(sink + shifted)
    return sizes[jax.random.permutation(jax.random.fold_in(key, 2), count)]


def normal_values(own_key, dims, deviation, bound, shards=(), kind=jnp.bfloat16):
    result = deviation * jax.random.normal(own_key, dims, jnp.float32)
    if shards:
        result = result * steps_of(own_key, dims, shards, -0.22, 0.18)
    return jnp.clip(result, -bound, bound).astype(kind)


def setup_inputs(seed: int = 0) -> dict:
    splits = jax.random.split(jax.random.key(seed), 6)
    return {
        "doc_ids": jnp.searchsorted(jnp.cumsum(ragged(splits[0], DOCS, TOKENS, DOC_MAX, 2)), jnp.arange(TOKENS), side="right").astype(jnp.int32),
        "attn_queries": draw_attn_queries(jax.random.fold_in(splits[5], 71), 0),
        "attn_keys": draw_attn_keys(jax.random.fold_in(splits[5], 71), 0),
        "attn_values": normal_values(splits[3], (TOKENS, HEADS * HEAD_DIM), 1.0, 6.0, ((0, 128),)),
        "attn_cot": normal_values(splits[4], (TOKENS, HEADS * HEAD_DIM), 1.0, 6.0, ((0, 128),)),
    }


NEG = -1.0e30


def attention_all(doc_ids, attn_queries, attn_keys, attn_values, attn_cot):
    reach = SPAN_SH * TOK_DEV
    window = reach + TOK_DEV
    score_scale = HEAD_DIM ** -0.5
    block_total = TOKENS // TOK_DEV
    key_doc = jnp.concatenate([jnp.full((reach,), -1, jnp.int32), doc_ids])
    key_pos = jnp.arange(TOKENS + reach, dtype=jnp.int32) - reach

    def one_head(head_id):
        start = head_id * HEAD_DIM
        query_head = lax.dynamic_slice_in_dim(attn_queries, start, HEAD_DIM, 1)
        cot_head = lax.dynamic_slice_in_dim(attn_cot, start, HEAD_DIM, 1)
        front = jnp.zeros((reach, HEAD_DIM), jnp.bfloat16)
        key_head = jnp.concatenate([front, lax.dynamic_slice_in_dim(attn_keys, start, HEAD_DIM, 1)], 0)
        value_head = jnp.concatenate([front, lax.dynamic_slice_in_dim(attn_values, start, HEAD_DIM, 1)], 0)

        def one_block(carry, block_id):
            grad_keys, grad_values = carry
            first = block_id * TOK_DEV
            query_part = lax.dynamic_slice_in_dim(query_head, first, TOK_DEV, 0)
            cot_part = lax.dynamic_slice_in_dim(cot_head, first, TOK_DEV, 0)
            key_part = lax.dynamic_slice_in_dim(key_head, first, window, 0)
            value_part = lax.dynamic_slice_in_dim(value_head, first, window, 0)
            query_doc = lax.dynamic_slice_in_dim(doc_ids, first, TOK_DEV, 0)
            query_pos = first + jnp.arange(TOK_DEV, dtype=jnp.int32)
            part_doc = lax.dynamic_slice_in_dim(key_doc, first, window, 0)
            part_pos = lax.dynamic_slice_in_dim(key_pos, first, window, 0)
            pair_mask = (part_doc[None, :] == query_doc[:, None]) & (part_pos[None, :] <= query_pos[:, None])
            raw_scores = jnp.dot(query_part, key_part.T, preferred_element_type=jnp.float32) * score_scale
            raw_scores = jnp.where(pair_mask, raw_scores, NEG)
            row_peak = jnp.max(raw_scores, axis=1)
            expo = jnp.exp(raw_scores - row_peak[:, None])
            denominator = jnp.sum(expo, axis=1)
            weight = (expo / denominator[:, None]).astype(jnp.bfloat16)
            out_part = jnp.dot(weight, value_part, preferred_element_type=jnp.float32).astype(jnp.bfloat16)
            dweight = jnp.dot(cot_part, value_part.T, preferred_element_type=jnp.float32)
            rowdot = jnp.sum(weight.astype(jnp.float32) * dweight, axis=1)
            dscore = (weight.astype(jnp.float32) * (dweight - rowdot[:, None])).astype(jnp.bfloat16)
            query_part_grad = (score_scale * jnp.dot(dscore, key_part, preferred_element_type=jnp.float32)).astype(jnp.bfloat16)
            key_term = score_scale * jnp.dot(dscore.T, query_part, preferred_element_type=jnp.float32)
            value_term = jnp.dot(weight.T, cot_part, preferred_element_type=jnp.float32)
            grad_keys = lax.dynamic_update_slice_in_dim(grad_keys, lax.dynamic_slice_in_dim(grad_keys, first, window, 0) + key_term, first, 0)
            grad_values = lax.dynamic_update_slice_in_dim(grad_values, lax.dynamic_slice_in_dim(grad_values, first, window, 0) + value_term, first, 0)
            return (grad_keys, grad_values), (out_part, query_part_grad)

        start_carry = (jnp.zeros((TOKENS + reach, HEAD_DIM), jnp.float32), jnp.zeros((TOKENS + reach, HEAD_DIM), jnp.float32))
        final_carry, block_results = lax.scan(one_block, start_carry, jnp.arange(block_total, dtype=jnp.int32))
        out_head = block_results[0].reshape(TOKENS, HEAD_DIM)
        query_grad_head = block_results[1].reshape(TOKENS, HEAD_DIM)
        key_grad_head = final_carry[0][reach:].astype(jnp.bfloat16)
        value_grad_head = final_carry[1][reach:].astype(jnp.bfloat16)
        return out_head, query_grad_head, key_grad_head, value_grad_head

    results = lax.map(one_head, jnp.arange(HEADS, dtype=jnp.int32))
    merged = [jnp.moveaxis(item, 0, 1).reshape(TOKENS, HEADS * HEAD_DIM) for item in results]
    return merged[0], merged[1], merged[2], merged[3]


def reference(doc_ids, attn_queries, attn_keys, attn_values, attn_cot):
    attn_out, query_grad, key_grad, value_grad = attention_all(doc_ids, attn_queries, attn_keys, attn_values, attn_cot)
    return (attn_out, query_grad, key_grad, value_grad)
```

```python
import functools

import jax
import jax.numpy as jnp
from jax import lax
from jax.experimental import pallas as pl
from jax.experimental.pallas import tpu as pltpu
from jax.sharding import PartitionSpec as P

MESH = pl.DeviceIdType.MESH
HEAD = 128
ROW = 8
CHAN = 4
TOK = 256
PIECE = 64
SPAN = ROW * TOK
HALO = 1024
KEYS = SPAN + HALO
PAIR = 2 * HEAD
LOG2E = 1.4426950408889634
NEG = -1e30
F32 = jnp.float32
BF16 = jnp.bfloat16
DOCS = 16


def place():
    shard = lax.axis_index("seq")
    plane = lax.axis_index("chan")
    spot = lax.rem(shard, ROW)
    return shard - spot, spot, plane


def wait_bytes(ref, sem):
    pltpu.make_async_copy(ref, ref, sem).wait()


def gather_kernel(rows_total, q, k, v, g, kv, qg, send_sem, recv_sem, up_send, up_recv):
    base, spot, plane = place()
    half = spot // 4
    above = (lax.rem(base + ROW, rows_total) + spot, plane)
    below = (lax.rem(base + rows_total - ROW, rows_total) + spot, plane)
    bar = pltpu.get_barrier_semaphore()
    for i in range(ROW):
        for j in range(CHAN):
            if i or j:
                peer = (base + lax.rem(spot + i, ROW), lax.rem(plane + j, CHAN))
                pl.semaphore_signal(bar, inc=1, device_id=peer, device_id_type=MESH)
    pl.semaphore_signal(bar, inc=1, device_id=above, device_id_type=MESH)
    pl.semaphore_signal(bar, inc=1, device_id=below, device_id_type=MESH)
    pl.semaphore_wait(bar, ROW * CHAN + 1)

    start = spot * TOK + plane * PIECE

    def columns(i, j):
        pair = lax.rem(plane + j, CHAN) * ROW + lax.rem(spot + i, ROW)
        return pl.ds(pl.multiple_of(pair * PAIR, PAIR), PAIR)

    def send(src, dst, t):
        pltpu.make_async_copy(src.at[:, columns(0, 0)], dst, recv_sem.at[t, half]).start()
        for i in range(ROW):
            for j in range(CHAN):
                if i or j:
                    pltpu.make_async_remote_copy(
                        src_ref=src.at[:, columns(i, j)],
                        dst_ref=dst,
                        send_sem=send_sem.at[t],
                        recv_sem=recv_sem.at[t, half],
                        device_id=(base + lax.rem(spot + i, ROW), lax.rem(plane + j, CHAN)),
                        device_id_type=MESH,
                    ).start()

    def rows(offset):
        return pl.ds(pl.multiple_of(offset + start, PIECE), PIECE)

    def raise_half(t):
        wait_bytes(kv.at[t, pl.ds(2 * HALO, HALO), :], recv_sem.at[t, 1])
        up = pltpu.make_async_remote_copy(
            src_ref=kv.at[t, pl.ds(2 * HALO, HALO), :],
            dst_ref=kv.at[t, pl.ds(0, HALO), :],
            send_sem=up_send.at[t],
            recv_sem=up_recv.at[t],
            device_id=above,
            device_id_type=MESH,
        )
        up.start()
        return up

    send(k, kv.at[0, rows(HALO), :], 0)
    send(v, kv.at[1, rows(HALO), :], 1)
    up_keys = raise_half(0)
    send(q, qg.at[0, rows(0), :], 2)
    up_values = raise_half(1)
    send(g, qg.at[1, rows(0), :], 3)
    for t in range(2):
        wait_bytes(kv.at[t, pl.ds(HALO, HALO), :], recv_sem.at[t, 0])
        wait_bytes(qg.at[t, pl.ds(0, HALO), :], recv_sem.at[2 + t, 0])
        wait_bytes(qg.at[t, pl.ds(HALO, HALO), :], recv_sem.at[2 + t, 1])
    for t in range(4):
        wait_bytes(qg.at[0, pl.ds(0, (ROW * CHAN - 1) * PIECE), :], send_sem.at[t])
    up_keys.wait()
    up_values.wait()


def gather_inputs(rows_total, q, k, v, g):
    any_space = pl.BlockSpec(memory_space=pl.ANY)
    return pl.pallas_call(
        functools.partial(gather_kernel, rows_total),
        out_shape=(
            jax.ShapeDtypeStruct((2, KEYS, PAIR), BF16),
            jax.ShapeDtypeStruct((2, SPAN, PAIR), BF16),
        ),
        in_specs=[any_space] * 4,
        out_specs=(any_space, any_space),
        scratch_shapes=[
            pltpu.SemaphoreType.DMA((4,)),
            pltpu.SemaphoreType.DMA((4, 2)),
            pltpu.SemaphoreType.DMA((2,)),
            pltpu.SemaphoreType.DMA((2,)),
        ],
        compiler_params=pltpu.CompilerParams(collective_id=0, has_side_effects=True),
        name="gather_inputs",
    )(q, k, v, g)


def dot(a, b, ca, cb):
    return lax.dot_general(a, b, (((ca,), (cb,)), ((), ())), preferred_element_type=F32)


def attention_kernel(docs_s, docs, kv, qg, og, dkv, scores, weights, keys_t, values_t, dk_acc, dv_acc, limits):
    base = lax.axis_index("seq") // ROW * SPAN
    scale = HEAD ** -0.5
    log_scale = scale * LOG2E

    all_docs = docs[...]
    first_line = base // HEAD
    own = docs[pl.ds(pl.multiple_of(first_line, 16), SPAN // HEAD), :]
    starts = jnp.zeros_like(own)
    for d in range(1, DOCS):
        below = jnp.where(all_docs < d, 1.0, 0.0)
        count = jnp.sum(jnp.sum(below, axis=0, keepdims=True), axis=1, keepdims=True)
        starts = jnp.where(own == d, jnp.broadcast_to(count.astype(jnp.int32), own.shape), starts)
    limits[...] = starts - (base - HALO)

    for b in range(KEYS // TOK):
        span = pl.ds(b * TOK, TOK)
        keys_t[:, span] = kv[0, span, :].T
        values_t[:, span] = kv[1, span, :].T
    dk_acc[...] = jnp.zeros_like(dk_acc)
    dv_acc[...] = jnp.zeros_like(dv_acc)

    heads = [pl.ds(h * HEAD, HEAD) for h in range(2)]
    key_iota = lax.broadcasted_iota(jnp.int32, (TOK, TOK), 0)
    diagonal = key_iota <= lax.broadcasted_iota(jnp.int32, (TOK, TOK), 1)

    def one_block(b, carry):
        first = base + b * TOK
        doc = docs_s[first]
        reach = jnp.int32(0)
        for o in range(1, 5):
            spot = first - 1 - (o - 1) * TOK
            hit = (spot >= 0) & (docs_s[jnp.maximum(spot, 0)] == doc)
            reach = reach + hit.astype(jnp.int32)
        rows = pl.ds(pl.multiple_of(b * TOK, TOK), TOK)
        low = jnp.concatenate([limits[pl.ds(2 * b, 1), :], limits[pl.ds(2 * b + 1, 1), :]], axis=1)
        queries = [qg[0, rows, heads[h]] for h in range(2)]
        cots = [qg[1, rows, heads[h]] for h in range(2)]

        def key_rows(o):
            return pl.ds(pl.multiple_of((b + 4 - o) * TOK, TOK), TOK)

        def masked(o, h):
            raw = dot(kv[0, key_rows(o), heads[h]], queries[h], 1, 1)
            return jnp.where(key_iota + (b + 4 - o) * TOK >= low, raw, NEG)

        peaks = []
        for h in range(2):
            part = jnp.where(diagonal, masked(0, h), NEG)
            scores[h, 0] = part
            peaks.append(jnp.max(part, axis=0, keepdims=True))

        def sweep_scores(o, peaks):
            out = []
            for h in range(2):
                part = masked(o, h)
                scores[h, o] = part
                out.append(jnp.maximum(peaks[h], jnp.max(part, axis=0, keepdims=True)))
            return tuple(out)

        peaks = lax.fori_loop(1, reach + 1, sweep_scores, tuple(peaks))
        shifts = [peak * log_scale for peak in peaks]

        def sweep_weights(o, state):
            out = []
            for h in range(2):
                total, mixed = state[h]
                expo = jnp.exp2(scores[h, o] * log_scale - shifts[h])
                small = expo.astype(BF16)
                weights[h, o] = small
                total = total + jnp.sum(expo, axis=0, keepdims=True)
                mixed = mixed + dot(values_t[heads[h], key_rows(o)], small, 1, 0)
                out.append((total, mixed))
            return tuple(out)

        zero = (jnp.zeros((1, TOK), F32), jnp.zeros((HEAD, TOK), F32))
        state = lax.fori_loop(0, reach + 1, sweep_weights, (zero, zero))
        tails = []
        for h in range(2):
            total, mixed = state[h]
            inverse = 1.0 / total
            mixed = mixed * inverse
            og[0, rows, heads[h]] = mixed.T.astype(BF16)
            cot_t = (cots[h].astype(F32).T * inverse).astype(BF16)
            rowdot = jnp.sum(cot_t.astype(F32) * mixed, axis=0, keepdims=True)
            tails.append((cot_t, cot_t.T, rowdot))

        def sweep_grads(o, grads):
            out = []
            keys = key_rows(o)
            for h in range(2):
                cot_t, cot, rowdot = tails[h]
                weight = weights[h, o]
                dweight = dot(kv[1, keys, heads[h]], cot_t, 1, 0)
                dscore = (weight.astype(F32) * (dweight - rowdot)).astype(BF16)
                dv_acc[keys, heads[h]] += dot(weight, cot, 1, 0)
                dk_acc[keys, heads[h]] += dot(dscore, queries[h], 1, 0)
                out.append(grads[h] + dot(keys_t[heads[h], keys], dscore, 1, 0))
            return tuple(out)

        blank = jnp.zeros((HEAD, TOK), F32)
        grads = lax.fori_loop(0, reach + 1, sweep_grads, (blank, blank))
        for h in range(2):
            og[1, rows, heads[h]] = (grads[h] * scale).T.astype(BF16)
        return carry

    lax.fori_loop(0, ROW, one_block, 0)
    for b in range(KEYS // TOK):
        span = pl.ds(b * TOK, TOK)
        dkv[0, span, :] = (dk_acc[span, :] * scale).astype(BF16)
        dkv[1, span, :] = dv_acc[span, :].astype(BF16)


def attention(docs, kv, qg):
    vmem = pl.BlockSpec(memory_space=pltpu.VMEM)
    return pl.pallas_call(
        attention_kernel,
        out_shape=(
            jax.ShapeDtypeStruct((2, SPAN, PAIR), BF16),
            jax.ShapeDtypeStruct((2, KEYS, PAIR), BF16),
        ),
        in_specs=[pl.BlockSpec(memory_space=pltpu.SMEM), vmem, vmem, vmem],
        out_specs=(vmem, vmem),
        scratch_shapes=[
            pltpu.VMEM((2, 5, TOK, TOK), F32),
            pltpu.VMEM((2, 5, TOK, TOK), BF16),
            pltpu.VMEM((PAIR, KEYS), BF16),
            pltpu.VMEM((PAIR, KEYS), BF16),
            pltpu.VMEM((KEYS, PAIR), F32),
            pltpu.VMEM((KEYS, PAIR), F32),
            pltpu.VMEM((SPAN // HEAD, HEAD), jnp.int32),
        ],
        compiler_params=pltpu.CompilerParams(vmem_limit_bytes=48 << 20),
        name="attention_rows",
    )(docs, docs.reshape(-1, HEAD), kv, qg)


def scatter_kernel(rows_total, og, dkv, o0, o1, o2, o3, far, near, send_sem, recv_sem, down_send, down_recv, local_sem):
    base, spot, plane = place()
    above = (lax.rem(base + ROW, rows_total) + spot, plane)
    below = (lax.rem(base + rows_total - ROW, rows_total) + spot, plane)
    bar = pltpu.get_barrier_semaphore()
    for i in range(1, ROW):
        peer = (base + lax.rem(spot + i, ROW), plane)
        pl.semaphore_signal(bar, inc=1, device_id=peer, device_id_type=MESH)
    pl.semaphore_signal(bar, inc=1, device_id=above, device_id_type=MESH)
    pl.semaphore_signal(bar, inc=1, device_id=below, device_id_type=MESH)
    pl.semaphore_wait(bar, ROW + 1)

    downs = []
    locals_ = []
    for t in range(2):
        down = pltpu.make_async_remote_copy(
            src_ref=dkv.at[t, pl.ds(0, HALO), :],
            dst_ref=far.at[t],
            send_sem=down_send.at[t],
            recv_sem=down_recv.at[t],
            device_id=below,
            device_id_type=MESH,
        )
        down.start()
        downs.append(down)
        copy = pltpu.make_async_copy(dkv.at[t, pl.ds(2 * HALO, HALO), :], near.at[t], local_sem.at[t])
        copy.start()
        locals_.append(copy)

    outs = (o0, o1, o2, o3)
    columns = pl.ds(pl.multiple_of(spot * PAIR, PAIR), PAIR)

    def send(src, t, i, other):
        dst = outs[t].at[:, columns]
        if i == 0:
            pltpu.make_async_copy(src, dst, recv_sem.at[t]).start()
        else:
            pltpu.make_async_remote_copy(
                src_ref=src,
                dst_ref=dst,
                send_sem=send_sem.at[t],
                recv_sem=recv_sem.at[t],
                device_id=(base + other, plane),
                device_id_type=MESH,
            ).start()

    def rows(offset):
        return pl.ds(pl.multiple_of(offset, TOK), TOK)

    for t in range(2):
        for i in range(ROW):
            other = lax.rem(spot + i, ROW)
            send(og.at[t, rows(other * TOK), :], t, i, other)
    for t in range(2):
        for i in range(ROW):
            other = lax.rem(spot + i, ROW)

            @pl.when(other < 4)
            def _():
                send(dkv.at[t, rows(HALO + other * TOK), :], 2 + t, i, other)

    for t in range(2):
        locals_[t].wait()
        downs[t].wait()
        for b in range(4):
            span = pl.ds(b * TOK, TOK)
            near[t, span, :] = (near[t, span, :].astype(F32) + far[t, span, :].astype(F32)).astype(BF16)
        for i in range(ROW):
            other = lax.rem(spot + i, ROW)

            @pl.when(other >= 4)
            def _():
                send(near.at[t, rows((other - 4) * TOK), :], 2 + t, i, other)

    for t in range(4):
        wait_bytes(outs[t], recv_sem.at[t])
        wait_bytes(og.at[0, pl.ds(0, (ROW - 1) * TOK), :], send_sem.at[t])


def scatter_outputs(rows_total, og, dkv):
    any_space = pl.BlockSpec(memory_space=pl.ANY)
    return pl.pallas_call(
        functools.partial(scatter_kernel, rows_total),
        out_shape=tuple(jax.ShapeDtypeStruct((TOK, ROW * PAIR), BF16) for _ in range(4)),
        in_specs=[any_space] * 2,
        out_specs=(any_space,) * 4,
        scratch_shapes=[
            pltpu.VMEM((2, HALO, PAIR), BF16),
            pltpu.VMEM((2, HALO, PAIR), BF16),
            pltpu.SemaphoreType.DMA((4,)),
            pltpu.SemaphoreType.DMA((4,)),
            pltpu.SemaphoreType.DMA((2,)),
            pltpu.SemaphoreType.DMA((2,)),
            pltpu.SemaphoreType.DMA((2,)),
        ],
        compiler_params=pltpu.CompilerParams(collective_id=1, has_side_effects=True),
        name="scatter_outputs",
    )(og, dkv)


def solution(mesh):
    rows_total = mesh.shape["seq"]

    def on_device(doc_ids, attn_queries, attn_keys, attn_values, attn_cot):
        kv, qg = gather_inputs(rows_total, attn_queries, attn_keys, attn_values, attn_cot)
        og, dkv = attention(doc_ids, kv, qg)
        attn_out, query_grad, key_grad, value_grad = scatter_outputs(rows_total, og, dkv)
        return attn_out, query_grad, key_grad, value_grad

    tokens = P(("seq", "chan"), None)
    return jax.shard_map(
        on_device,
        mesh=mesh,
        in_specs=(P(), tokens, tokens, tokens, tokens),
        out_specs=(P("seq", "chan"),) * 4,
        check_vma=False,
    )
```

```python
import functools

import jax
import jax.numpy as jnp
from jax import lax
from jax.experimental import pallas as pl
from jax.experimental.pallas import tpu as pltpu
from jax.sharding import PartitionSpec as P

MESH = pl.DeviceIdType.MESH
HEAD = 128
ROW = 8
CHAN = 4
TOK = 256
PIECE = 64
SPAN = ROW * TOK
HALO = 1024
KEYS = SPAN + HALO
PAIR = 2 * HEAD
LOG2E = 1.4426950408889634
NEG = -1e30
F32 = jnp.float32
BF16 = jnp.bfloat16
DOCS = 16


def place():
    shard = lax.axis_index("seq")
    plane = lax.axis_index("chan")
    spot = lax.rem(shard, ROW)
    return shard - spot, spot, plane


def wait_bytes(ref, sem):
    pltpu.make_async_copy(ref, ref, sem).wait()


def dot(a, b):
    return jnp.dot(a, b, preferred_element_type=F32)


def whole_kernel(
    rows_total, q, k, v, g, docs, land,
    kv, qg, og, dkv, far, scores, weights, keys_t, values_t, dk_acc, dv_acc, limits,
    send_sem, recv_sem, up_send, up_recv, down_send, down_recv, home_send, home_recv,
):
    base, spot, plane = place()
    half = spot // 4
    above = (lax.rem(base + ROW, rows_total) + spot, plane)
    below = (lax.rem(base + rows_total - ROW, rows_total) + spot, plane)
    scale = HEAD ** -0.5
    log_scale = scale * LOG2E

    bar = pltpu.get_barrier_semaphore()
    for i in range(ROW):
        for j in range(CHAN):
            if i or j:
                peer = (base + lax.rem(spot + i, ROW), lax.rem(plane + j, CHAN))
                pl.semaphore_signal(bar, inc=1, device_id=peer, device_id_type=MESH)
    pl.semaphore_signal(bar, inc=1, device_id=above, device_id_type=MESH)
    pl.semaphore_signal(bar, inc=1, device_id=below, device_id_type=MESH)
    pl.semaphore_wait(bar, ROW * CHAN + 1)

    def send(src, t, h):
        offset = spot * TOK + plane * PIECE + (HALO if t < 2 else 0)
        rows = pl.ds(pl.multiple_of(offset, PIECE), PIECE)
        dst = (kv if t < 2 else qg).at[t % 2, h, rows, :]
        arrival = recv_sem.at[t, h, half]

        def columns(room, floor):
            first = (floor * ROW + room) * PAIR + h * HEAD
            return pl.ds(pl.multiple_of(first, HEAD), HEAD)

        pltpu.make_async_copy(src.at[:, columns(spot, plane)], dst, arrival).start()

        def one(n, carry):
            room = lax.rem(spot + n // CHAN, ROW)
            floor = lax.rem(plane + lax.rem(n, CHAN), CHAN)
            pltpu.make_async_remote_copy(
                src_ref=src.at[:, columns(room, floor)],
                dst_ref=dst,
                send_sem=send_sem.at[t, h],
                recv_sem=arrival,
                device_id=(base + room, floor),
                device_id_type=MESH,
            ).start()
            return carry

        lax.fori_loop(1, ROW * CHAN, one, 0)

    def climb(t, h):
        return pltpu.make_async_remote_copy(
            src_ref=kv.at[t, h, pl.ds(2 * HALO, HALO), :],
            dst_ref=kv.at[t, h, pl.ds(0, HALO), :],
            send_sem=up_send.at[t, h],
            recv_sem=up_recv.at[t, h],
            device_id=above,
            device_id_type=MESH,
        )

    def raise_half(t, h):
        wait_bytes(kv.at[t, h, pl.ds(2 * HALO, HALO), :], recv_sem.at[t, h, 1])
        climb(t, h).start()

    def arrive(h):
        for t in range(2):
            wait_bytes(kv.at[t, h, pl.ds(HALO, HALO), :], recv_sem.at[t, h, 0])
            wait_bytes(qg.at[t, h, pl.ds(0, HALO), :], recv_sem.at[2 + t, h, 0])
            wait_bytes(qg.at[t, h, pl.ds(HALO, HALO), :], recv_sem.at[2 + t, h, 1])
        for t in range(2):
            climb(t, h).wait_recv()

    def drop(t, h):
        return pltpu.make_async_remote_copy(
            src_ref=dkv.at[t, h, pl.ds(0, HALO), :],
            dst_ref=far.at[t, h],
            send_sem=down_send.at[t, h],
            recv_sem=down_recv.at[t, h],
            device_id=below,
            device_id_type=MESH,
        )

    def go_home(src, t, h, i):
        other = lax.rem(spot + i, ROW)
        dst = land.at[t, h, spot]
        if i == 0:
            pltpu.make_async_copy(src, dst, home_recv.at[t, h]).start()
        else:
            pltpu.make_async_remote_copy(
                src_ref=src,
                dst_ref=dst,
                send_sem=home_send.at[t, h],
                recv_sem=home_recv.at[t, h],
                device_id=(base + other, plane),
                device_id_type=MESH,
            ).start()

    def rows_at(offset):
        return pl.ds(pl.multiple_of(offset, TOK), TOK)

    def home_queries(h):
        for t in range(2):
            for i in range(ROW):
                go_home(og.at[t, h, rows_at(lax.rem(spot + i, ROW) * TOK), :], t, h, i)

    def home_keys(h, upper):
        for t in range(2):
            for i in range(ROW):
                other = lax.rem(spot + i, ROW)

                @pl.when((other >= 4) if upper else (other < 4))
                def _():
                    go_home(dkv.at[t, h, rows_at(HALO + other * TOK), :], 2 + t, h, i)

    def set_limits():
        all_docs = docs[...]
        own = docs[pl.ds(pl.multiple_of(base * (TOK // HEAD), 16), SPAN // HEAD), :]
        starts = jnp.zeros_like(own)
        for d in range(1, DOCS):
            below_d = jnp.where(all_docs < d, 1.0, 0.0)
            count = jnp.sum(jnp.sum(below_d, axis=0, keepdims=True), axis=1, keepdims=True)
            starts = jnp.where(own == d, jnp.broadcast_to(count.astype(jnp.int32), own.shape), starts)
        limits[...] = starts - (base * TOK - HALO)

    key_iota = lax.broadcasted_iota(jnp.int32, (TOK, TOK), 0)
    diagonal = key_iota <= lax.broadcasted_iota(jnp.int32, (TOK, TOK), 1)
    reach = HALO // TOK + 1

    def prepare(h):
        for b in range(KEYS // TOK):
            span = pl.ds(b * TOK, TOK)
            keys_t[:, span] = kv[0, h, span, :].T
            values_t[:, span] = kv[1, h, span, :].T
        dk_acc[...] = jnp.zeros_like(dk_acc)
        dv_acc[...] = jnp.zeros_like(dv_acc)

    def attend(h, first, last):
        def one_block(b, carry):
            rows = rows_at(b * TOK)
            low = jnp.concatenate([limits[pl.ds(2 * b, 1), :], limits[pl.ds(2 * b + 1, 1), :]], axis=1)
            queries = qg[0, h, rows, :]
            queries_t = queries.T
            cot_raw_t = qg[1, h, rows, :].T

            def key_rows(o):
                return rows_at((b + reach - 1 - o) * TOK)

            peak = jnp.full((1, TOK), NEG, F32)
            for o in range(reach):
                raw = dot(kv[0, h, key_rows(o), :], queries_t)
                inside = key_iota >= low - (b + reach - 1 - o) * TOK
                if o == 0:
                    inside = inside & diagonal
                raw = jnp.where(inside, raw, NEG)
                scores[o] = raw
                peak = jnp.maximum(peak, jnp.max(raw, axis=0, keepdims=True))
            shift = peak * log_scale
            total = jnp.zeros((1, TOK), F32)
            mixed = jnp.zeros((HEAD, TOK), F32)
            for o in range(reach):
                expo = jnp.exp2(scores[o] * log_scale - shift)
                small = expo.astype(BF16)
                weights[o] = small
                total = total + jnp.sum(expo, axis=0, keepdims=True)
                mixed = mixed + dot(values_t[:, key_rows(o)], small)
            inverse = 1.0 / total
            mixed = mixed * inverse
            og[0, h, rows, :] = mixed.T.astype(BF16)
            cot_t = (cot_raw_t.astype(F32) * inverse).astype(BF16)
            rowdot = jnp.sum(cot_t.astype(F32) * mixed, axis=0, keepdims=True)
            cot = cot_t.T
            grad = jnp.zeros((HEAD, TOK), F32)
            for o in range(reach):
                keys = key_rows(o)
                weight = weights[o]
                dweight = dot(kv[1, h, keys, :], cot_t)
                dscore = (weight.astype(F32) * (dweight - rowdot)).astype(BF16)
                dv_acc[keys, :] += dot(weight, cot)
                dk_acc[keys, :] += dot(dscore, queries)
                grad = grad + dot(keys_t[:, keys], dscore)
            og[1, h, rows, :] = (grad * scale).T.astype(BF16)
            return carry

        lax.fori_loop(first, last, one_block, 0)

    def settle(h, first, last):
        for b in range(first, last):
            span = pl.ds(b * TOK, TOK)
            dkv[0, h, span, :] = (dk_acc[span, :] * scale).astype(BF16)
            dkv[1, h, span, :] = dv_acc[span, :].astype(BF16)

    def join(h):
        for t in range(2):
            drop(t, h).wait_recv()
            for b in range(4):
                span = pl.ds(2 * HALO + b * TOK, TOK)
                near = dkv[t, h, span, :].astype(F32)
                dkv[t, h, span, :] = (near + far[t, h, pl.ds(b * TOK, TOK), :].astype(F32)).astype(BF16)
        home_keys(h, True)

    send(k, 0, 0)
    send(v, 1, 0)
    set_limits()
    raise_half(0, 0)
    send(q, 2, 0)
    raise_half(1, 0)
    send(g, 3, 0)
    send(k, 0, 1)
    send(v, 1, 1)
    send(q, 2, 1)
    send(g, 3, 1)
    arrive(0)
    prepare(0)
    attend(0, 0, 4)
    raise_half(0, 1)
    settle(0, 0, 4)
    for t in range(2):
        drop(t, 0).start()
    attend(0, 4, 8)
    raise_half(1, 1)
    settle(0, 4, 12)
    home_queries(0)
    home_keys(0, False)
    arrive(1)
    prepare(1)
    attend(1, 0, 4)
    settle(1, 0, 4)
    for t in range(2):
        drop(t, 1).start()
    join(0)
    attend(1, 4, 8)
    settle(1, 4, 12)
    home_queries(1)
    home_keys(1, False)
    join(1)

    for h in range(2):
        for t in range(2):
            climb(t, h).wait_send()
            drop(t, h).wait_send()
        for t in range(4):
            wait_bytes(qg.at[0, 0, pl.ds(0, (ROW * CHAN - 1) * PIECE), :], send_sem.at[t, h])
            wait_bytes(og.at[0, 0, pl.ds(0, (ROW - 1) * TOK), :], home_send.at[t, h])
            wait_bytes(land.at[t, h], home_recv.at[t, h])


def whole(rows_total, docs, q, k, v, g):
    any_space = pl.BlockSpec(memory_space=pl.ANY)
    vmem = pl.BlockSpec(memory_space=pltpu.VMEM)
    dma = pltpu.SemaphoreType.DMA
    return pl.pallas_call(
        functools.partial(whole_kernel, rows_total),
        out_shape=jax.ShapeDtypeStruct((4, 2, ROW, TOK, HEAD), BF16),
        in_specs=[pl.BlockSpec(memory_space=pltpu.MemorySpace.HBM)] * 4 + [vmem],
        out_specs=pl.BlockSpec(memory_space=pltpu.MemorySpace.HBM),
        scratch_shapes=[
            pltpu.VMEM((2, 2, KEYS, HEAD), BF16),
            pltpu.VMEM((2, 2, SPAN, HEAD), BF16),
            pltpu.VMEM((2, 2, SPAN, HEAD), BF16),
            pltpu.VMEM((2, 2, KEYS, HEAD), BF16),
            pltpu.VMEM((2, 2, HALO, HEAD), BF16),
            pltpu.VMEM((5, TOK, TOK), F32),
            pltpu.VMEM((5, TOK, TOK), BF16),
            pltpu.VMEM((HEAD, KEYS), BF16),
            pltpu.VMEM((HEAD, KEYS), BF16),
            pltpu.VMEM((KEYS, HEAD), F32),
            pltpu.VMEM((KEYS, HEAD), F32),
            pltpu.VMEM((SPAN // HEAD, HEAD), jnp.int32),
            dma((4, 2)),
            dma((4, 2, 2)),
            dma((2, 2)),
            dma((2, 2)),
            dma((2, 2)),
            dma((2, 2)),
            dma((4, 2)),
            dma((4, 2)),
        ],
        compiler_params=pltpu.CompilerParams(
            collective_id=0, has_side_effects=True, vmem_limit_bytes=60 << 20
        ),
        name="whole_rows",
    )(q, k, v, g, docs.reshape(-1, HEAD))


def lay_kernel(land, o0, o1, o2, o3, sems):
    copies = []
    for t, out in enumerate((o0, o1, o2, o3)):
        for h in range(2):
            for r in range(ROW):
                lanes = pl.ds((2 * r + h) * HEAD, HEAD)
                copies.append(pltpu.make_async_copy(land.at[t, h, r], out.at[:, lanes], sems.at[t, h, r]))
    for copy in copies:
        copy.start()
    for copy in copies:
        copy.wait()


def lay_out(land):
    any_space = pl.BlockSpec(memory_space=pl.ANY)
    return pl.pallas_call(
        lay_kernel,
        out_shape=tuple(jax.ShapeDtypeStruct((TOK, ROW * PAIR), BF16) for _ in range(4)),
        in_specs=[pl.BlockSpec(memory_space=pltpu.MemorySpace.HBM)],
        out_specs=(any_space,) * 4,
        scratch_shapes=[pltpu.SemaphoreType.DMA((4, 2, ROW))],
        name="lay_out",
    )(land)


def solution(mesh):
    rows_total = mesh.shape["seq"]

    def on_device(doc_ids, attn_queries, attn_keys, attn_values, attn_cot):
        land = whole(rows_total, doc_ids, attn_queries, attn_keys, attn_values, attn_cot)
        return lay_out(land)

    tokens = P(("seq", "chan"), None)
    return jax.shard_map(
        on_device,
        mesh=mesh,
        in_specs=(P(), tokens, tokens, tokens, tokens),
        out_specs=(P("seq", "chan"),) * 4,
        check_vma=False,
    )
```

```python
import functools

import jax
import jax.numpy as jnp
from jax import lax
from jax.experimental import pallas as pl
from jax.experimental.pallas import tpu as pltpu
from jax.sharding import PartitionSpec as P

MESH = pl.DeviceIdType.MESH
HEAD = 128
ROW = 8
CHAN = 4
TOK = 256
PIECE = 64
SPAN = ROW * TOK
HALO = 1024
KEYS = SPAN + HALO
PAIR = 2 * HEAD
LOG2E = 1.4426950408889634
NEG = -1e30
F32 = jnp.float32
BF16 = jnp.bfloat16
DOCS = 16


def place():
    shard = lax.axis_index("seq")
    plane = lax.axis_index("chan")
    spot = lax.rem(shard, ROW)
    return shard - spot, spot, plane


def wait_bytes(ref, sem):
    pltpu.make_async_copy(ref, ref, sem).wait()


def dot(a, b):
    return jnp.dot(a, b, preferred_element_type=F32)


def whole_kernel(
    rows_total, q, k, v, g, docs, land,
    kv, qg, og, dkv, far, scores, weights, keys_t, values_t, dk_acc, dv_acc, limits,
    send_sem, recv_sem, up_send, up_recv, down_send, down_recv, home_send, home_recv,
):
    base, spot, plane = place()
    half = spot // 4
    above = (lax.rem(base + ROW, rows_total) + spot, plane)
    below = (lax.rem(base + rows_total - ROW, rows_total) + spot, plane)
    scale = HEAD ** -0.5
    log_scale = scale * LOG2E

    bar = pltpu.get_barrier_semaphore()
    for i in range(ROW):
        for j in range(CHAN):
            if i or j:
                peer = (base + lax.rem(spot + i, ROW), lax.rem(plane + j, CHAN))
                pl.semaphore_signal(bar, inc=1, device_id=peer, device_id_type=MESH)
    pl.semaphore_signal(bar, inc=1, device_id=above, device_id_type=MESH)
    pl.semaphore_signal(bar, inc=1, device_id=below, device_id_type=MESH)
    pl.semaphore_wait(bar, ROW * CHAN + 1)

    def send(src, t, h):
        offset = spot * TOK + plane * PIECE + (HALO if t < 2 else 0)
        rows = pl.ds(pl.multiple_of(offset, PIECE), PIECE)
        dst = (kv if t < 2 else qg).at[t % 2, h, rows, :]
        arrival = recv_sem.at[t, h, half]

        def columns(room, floor):
            first = (floor * ROW + room) * PAIR + h * HEAD
            return pl.ds(pl.multiple_of(first, HEAD), HEAD)

        pltpu.make_async_copy(src.at[:, columns(spot, plane)], dst, arrival).start()

        def one(n, carry):
            room = lax.rem(spot + n // CHAN, ROW)
            floor = lax.rem(plane + lax.rem(n, CHAN), CHAN)
            pltpu.make_async_remote_copy(
                src_ref=src.at[:, columns(room, floor)],
                dst_ref=dst,
                send_sem=send_sem.at[t, h],
                recv_sem=arrival,
                device_id=(base + room, floor),
                device_id_type=MESH,
            ).start()
            return carry

        lax.fori_loop(1, ROW * CHAN, one, 0)

    def climb(t, h):
        return pltpu.make_async_remote_copy(
            src_ref=kv.at[t, h, pl.ds(2 * HALO, HALO), :],
            dst_ref=kv.at[t, h, pl.ds(0, HALO), :],
            send_sem=up_send.at[t, h],
            recv_sem=up_recv.at[t, h],
            device_id=above,
            device_id_type=MESH,
        )

    def raise_half(t, h):
        wait_bytes(kv.at[t, h, pl.ds(2 * HALO, HALO), :], recv_sem.at[t, h, 1])
        climb(t, h).start()

    def arrive(h):
        for t in range(2):
            wait_bytes(kv.at[t, h, pl.ds(HALO, HALO), :], recv_sem.at[t, h, 0])
            wait_bytes(qg.at[t, h, pl.ds(0, HALO), :], recv_sem.at[2 + t, h, 0])
            wait_bytes(qg.at[t, h, pl.ds(HALO, HALO), :], recv_sem.at[2 + t, h, 1])
        for t in range(2):
            climb(t, h).wait_recv()

    def drop(t, h):
        return pltpu.make_async_remote_copy(
            src_ref=dkv.at[t, h, pl.ds(0, HALO), :],
            dst_ref=far.at[t, h],
            send_sem=down_send.at[t, h],
            recv_sem=down_recv.at[t, h],
            device_id=below,
            device_id_type=MESH,
        )

    def go_home(src, t, h, i):
        other = lax.rem(spot + i, ROW)
        dst = land.at[t, h, spot]
        if i == 0:
            pltpu.make_async_copy(src, dst, home_recv.at[t, h]).start()
        else:
            pltpu.make_async_remote_copy(
                src_ref=src,
                dst_ref=dst,
                send_sem=home_send.at[t, h],
                recv_sem=home_recv.at[t, h],
                device_id=(base + other, plane),
                device_id_type=MESH,
            ).start()

    def rows_at(offset):
        return pl.ds(pl.multiple_of(offset, TOK), TOK)

    def home_queries(h):
        for t in range(2):
            for i in range(ROW):
                go_home(og.at[t, h, rows_at(lax.rem(spot + i, ROW) * TOK), :], t, h, i)

    def home_keys(h, upper):
        for t in range(2):
            for i in range(ROW):
                other = lax.rem(spot + i, ROW)

                @pl.when((other >= 4) if upper else (other < 4))
                def _():
                    go_home(dkv.at[t, h, rows_at(HALO + other * TOK), :], 2 + t, h, i)

    def set_limits():
        all_docs = docs[...]
        own = docs[pl.ds(pl.multiple_of(base * (TOK // HEAD), 16), SPAN // HEAD), :]
        starts = jnp.zeros_like(own)
        for d in range(1, DOCS):
            below_d = jnp.where(all_docs < d, 1.0, 0.0)
            count = jnp.sum(jnp.sum(below_d, axis=0, keepdims=True), axis=1, keepdims=True)
            starts = jnp.where(own == d, jnp.broadcast_to(count.astype(jnp.int32), own.shape), starts)
        limits[...] = starts - (base * TOK - HALO)

    key_iota = lax.broadcasted_iota(jnp.int32, (TOK, TOK), 0)
    diagonal = key_iota <= lax.broadcasted_iota(jnp.int32, (TOK, TOK), 1)
    reach = HALO // TOK + 1

    def prepare(h):
        for b in range(KEYS // TOK):
            span = pl.ds(b * TOK, TOK)
            keys_t[:, span] = kv[0, h, span, :].T
            values_t[:, span] = kv[1, h, span, :].T
        dk_acc[...] = jnp.zeros_like(dk_acc)
        dv_acc[...] = jnp.zeros_like(dv_acc)

    def attend(h, first, last):
        def one_block(b, carry):
            rows = rows_at(b * TOK)
            low = jnp.concatenate([limits[pl.ds(2 * b, 1), :], limits[pl.ds(2 * b + 1, 1), :]], axis=1)
            queries = qg[0, h, rows, :]
            queries_t = queries.T
            cot_raw_t = qg[1, h, rows, :].T

            def key_rows(o):
                return rows_at((b + reach - 1 - o) * TOK)

            peak = jnp.full((1, TOK), NEG, F32)
            for o in range(reach):
                raw = dot(kv[0, h, key_rows(o), :], queries_t)
                inside = key_iota >= low - (b + reach - 1 - o) * TOK
                if o == 0:
                    inside = inside & diagonal
                raw = jnp.where(inside, raw, NEG)
                scores[o] = raw
                peak = jnp.maximum(peak, jnp.max(raw, axis=0, keepdims=True))
            shift = peak * log_scale
            total = jnp.zeros((1, TOK), F32)
            mixed = jnp.zeros((HEAD, TOK), F32)
            for o in range(reach):
                expo = jnp.exp2(scores[o] * log_scale - shift)
                small = expo.astype(BF16)
                weights[o] = small
                total = total + jnp.sum(expo, axis=0, keepdims=True)
                mixed = mixed + dot(values_t[:, key_rows(o)], small)
            inverse = 1.0 / total
            mixed = mixed * inverse
            og[0, h, rows, :] = mixed.T.astype(BF16)
            cot_t = (cot_raw_t.astype(F32) * inverse).astype(BF16)
            rowdot = jnp.sum(cot_t.astype(F32) * mixed, axis=0, keepdims=True)
            cot = cot_t.T
            grad = jnp.zeros((HEAD, TOK), F32)
            for o in range(reach):
                keys = key_rows(o)
                weight = weights[o]
                dweight = dot(kv[1, h, keys, :], cot_t)
                dscore = (weight.astype(F32) * (dweight - rowdot)).astype(BF16)
                dv_acc[keys, :] += dot(weight, cot)
                dk_acc[keys, :] += dot(dscore, queries)
                grad = grad + dot(keys_t[:, keys], dscore)
            og[1, h, rows, :] = (grad * scale).T.astype(BF16)
            return carry

        lax.fori_loop(first, last, one_block, 0)

    def settle(h, first, last):
        for b in range(first, last):
            span = pl.ds(b * TOK, TOK)
            dkv[0, h, span, :] = (dk_acc[span, :] * scale).astype(BF16)
            dkv[1, h, span, :] = dv_acc[span, :].astype(BF16)

    def join(h):
        for t in range(2):
            drop(t, h).wait_recv()
            for b in range(4):
                span = pl.ds(2 * HALO + b * TOK, TOK)
                near = dkv[t, h, span, :].astype(F32)
                dkv[t, h, span, :] = (near + far[t, h, pl.ds(b * TOK, TOK), :].astype(F32)).astype(BF16)
        home_keys(h, True)

    send(k, 0, 0)
    send(v, 1, 0)
    set_limits()
    raise_half(0, 0)
    send(q, 2, 0)
    raise_half(1, 0)
    send(g, 3, 0)
    send(k, 0, 1)
    send(v, 1, 1)
    send(q, 2, 1)
    send(g, 3, 1)
    arrive(0)
    prepare(0)
    attend(0, 0, 4)
    raise_half(0, 1)
    settle(0, 0, 4)
    for t in range(2):
        drop(t, 0).start()
    attend(0, 4, 8)
    raise_half(1, 1)
    settle(0, 4, 12)
    home_queries(0)
    home_keys(0, False)
    arrive(1)
    prepare(1)
    attend(1, 0, 4)
    settle(1, 0, 4)
    for t in range(2):
        drop(t, 1).start()
    join(0)
    attend(1, 4, 8)
    settle(1, 4, 12)
    home_queries(1)
    home_keys(1, False)
    join(1)

    for h in range(2):
        for t in range(2):
            climb(t, h).wait_send()
            drop(t, h).wait_send()
        for t in range(4):
            wait_bytes(qg.at[0, 0, pl.ds(0, (ROW * CHAN - 1) * PIECE), :], send_sem.at[t, h])
            wait_bytes(og.at[0, 0, pl.ds(0, (ROW - 1) * TOK), :], home_send.at[t, h])
            wait_bytes(land.at[t, h], home_recv.at[t, h])


def whole(rows_total, docs, q, k, v, g):
    any_space = pl.BlockSpec(memory_space=pl.ANY)
    vmem = pl.BlockSpec(memory_space=pltpu.VMEM)
    dma = pltpu.SemaphoreType.DMA
    return pl.pallas_call(
        functools.partial(whole_kernel, rows_total),
        out_shape=jax.ShapeDtypeStruct((4, 2, ROW, TOK, HEAD), BF16),
        in_specs=[pl.BlockSpec(memory_space=pltpu.MemorySpace.HBM)] * 4 + [vmem],
        out_specs=pl.BlockSpec(memory_space=pltpu.MemorySpace.HBM),
        scratch_shapes=[
            pltpu.VMEM((2, 2, KEYS, HEAD), BF16),
            pltpu.VMEM((2, 2, SPAN, HEAD), BF16),
            pltpu.VMEM((2, 2, SPAN, HEAD), BF16),
            pltpu.VMEM((2, 2, KEYS, HEAD), BF16),
            pltpu.VMEM((2, 2, HALO, HEAD), BF16),
            pltpu.VMEM((5, TOK, TOK), F32),
            pltpu.VMEM((5, TOK, TOK), BF16),
            pltpu.VMEM((HEAD, KEYS), BF16),
            pltpu.VMEM((HEAD, KEYS), BF16),
            pltpu.VMEM((KEYS, HEAD), F32),
            pltpu.VMEM((KEYS, HEAD), F32),
            pltpu.VMEM((SPAN // HEAD, HEAD), jnp.int32),
            dma((4, 2)),
            dma((4, 2, 2)),
            dma((2, 2)),
            dma((2, 2)),
            dma((2, 2)),
            dma((2, 2)),
            dma((4, 2)),
            dma((4, 2)),
        ],
        compiler_params=pltpu.CompilerParams(
            collective_id=0, has_side_effects=True, vmem_limit_bytes=60 << 20
        ),
        name="whole_rows",
    )(q, k, v, g, docs.reshape(-1, HEAD))


def lay_kernel(land, o0, o1, o2, o3):
    for t, out in enumerate((o0, o1, o2, o3)):
        for r in range(2):
            for h in range(2):
                out[:, pl.ds((2 * r + h) * HEAD, HEAD)] = land[t, h, r]


def lay_out(land):
    return pl.pallas_call(
        lay_kernel,
        grid=(ROW // 2,),
        out_shape=tuple(jax.ShapeDtypeStruct((TOK, ROW * PAIR), BF16) for _ in range(4)),
        in_specs=[pl.BlockSpec((4, 2, 2, TOK, HEAD), lambda r: (0, 0, r, 0, 0))],
        out_specs=tuple(pl.BlockSpec((TOK, 2 * PAIR), lambda r: (0, r)) for _ in range(4)),
        name="lay_out",
    )(land)


def solution(mesh):
    rows_total = mesh.shape["seq"]

    def on_device(doc_ids, attn_queries, attn_keys, attn_values, attn_cot):
        land = whole(rows_total, doc_ids, attn_queries, attn_keys, attn_values, attn_cot)
        return lay_out(land)

    tokens = P(("seq", "chan"), None)
    return jax.shard_map(
        on_device,
        mesh=mesh,
        in_specs=(P(), tokens, tokens, tokens, tokens),
        out_specs=(P("seq", "chan"),) * 4,
        check_vma=False,
    )
```

```python
import functools

import jax
import jax.numpy as jnp
from jax import lax
from jax.experimental import pallas as pl
from jax.experimental.pallas import tpu as pltpu
from jax.sharding import PartitionSpec as P

MESH = pl.DeviceIdType.MESH
HEAD = 128
ROW = 8
CHAN = 4
TOK = 256
PIECE = 64
SPAN = ROW * TOK
HALO = 1024
KEYS = SPAN + HALO
PAIR = 2 * HEAD
LOG2E = 1.4426950408889634
NEG = -1e30
F32 = jnp.float32
BF16 = jnp.bfloat16
DOCS = 16


def place():
    shard = lax.axis_index("seq")
    plane = lax.axis_index("chan")
    spot = lax.rem(shard, ROW)
    return shard - spot, spot, plane


def wait_bytes(ref, sem):
    pltpu.make_async_copy(ref, ref, sem).wait()


def dot(a, b):
    return jnp.dot(a, b, preferred_element_type=F32)


def whole_kernel(
    rows_total, q, k, v, g, docs_far, land,
    docs, kv, qg, og, dkv, far, scores, weights, keys_t, values_t, dk_acc, dv_acc, limits,
    send_sem, recv_sem, up_send, up_recv, down_send, down_recv, home_send, home_recv, docs_sem,
):
    base, spot, plane = place()
    half = spot // 4
    above = (lax.rem(base + ROW, rows_total) + spot, plane)
    below = (lax.rem(base + rows_total - ROW, rows_total) + spot, plane)
    scale = HEAD ** -0.5
    log_scale = scale * LOG2E

    fetch = pltpu.make_async_copy(docs_far, docs, docs_sem)
    fetch.start()
    bar = pltpu.get_barrier_semaphore()
    for i in range(ROW):
        for j in range(CHAN):
            if i or j:
                peer = (base + lax.rem(spot + i, ROW), lax.rem(plane + j, CHAN))
                pl.semaphore_signal(bar, inc=1, device_id=peer, device_id_type=MESH)
    pl.semaphore_signal(bar, inc=1, device_id=above, device_id_type=MESH)
    pl.semaphore_signal(bar, inc=1, device_id=below, device_id_type=MESH)
    pl.semaphore_wait(bar, ROW * CHAN + 1)

    def send(src, t, h):
        offset = spot * TOK + plane * PIECE + (HALO if t < 2 else 0)
        rows = pl.ds(pl.multiple_of(offset, PIECE), PIECE)
        dst = (kv if t < 2 else qg).at[t % 2, h, rows, :]
        arrival = recv_sem.at[t, h, half]

        def columns(room, floor):
            first = (floor * ROW + room) * PAIR + h * HEAD
            return pl.ds(pl.multiple_of(first, HEAD), HEAD)

        pltpu.make_async_copy(src.at[:, columns(spot, plane)], dst, arrival).start()

        def one(n, carry):
            room = lax.rem(spot + n // CHAN, ROW)
            floor = lax.rem(plane + lax.rem(n, CHAN), CHAN)
            pltpu.make_async_remote_copy(
                src_ref=src.at[:, columns(room, floor)],
                dst_ref=dst,
                send_sem=send_sem.at[t, h],
                recv_sem=arrival,
                device_id=(base + room, floor),
                device_id_type=MESH,
            ).start()
            return carry

        lax.fori_loop(1, ROW * CHAN, one, 0)

    def climb(t, h):
        return pltpu.make_async_remote_copy(
            src_ref=kv.at[t, h, pl.ds(2 * HALO, HALO), :],
            dst_ref=kv.at[t, h, pl.ds(0, HALO), :],
            send_sem=up_send.at[t, h],
            recv_sem=up_recv.at[t, h],
            device_id=above,
            device_id_type=MESH,
        )

    def raise_half(t, h):
        wait_bytes(kv.at[t, h, pl.ds(2 * HALO, HALO), :], recv_sem.at[t, h, 1])
        climb(t, h).start()

    def arrive(h):
        for t in range(2):
            wait_bytes(kv.at[t, h, pl.ds(HALO, HALO), :], recv_sem.at[t, h, 0])
            wait_bytes(qg.at[t, h, pl.ds(0, HALO), :], recv_sem.at[2 + t, h, 0])
            wait_bytes(qg.at[t, h, pl.ds(HALO, HALO), :], recv_sem.at[2 + t, h, 1])
        for t in range(2):
            climb(t, h).wait_recv()

    def drop(t, h):
        return pltpu.make_async_remote_copy(
            src_ref=dkv.at[t, h, pl.ds(0, HALO), :],
            dst_ref=far.at[t, h],
            send_sem=down_send.at[t, h],
            recv_sem=down_recv.at[t, h],
            device_id=below,
            device_id_type=MESH,
        )

    def go_home(src, t, h, i):
        other = lax.rem(spot + i, ROW)
        dst = land.at[t, h, spot]
        if i == 0:
            pltpu.make_async_copy(src, dst, home_recv.at[t, h]).start()
        else:
            pltpu.make_async_remote_copy(
                src_ref=src,
                dst_ref=dst,
                send_sem=home_send.at[t, h],
                recv_sem=home_recv.at[t, h],
                device_id=(base + other, plane),
                device_id_type=MESH,
            ).start()

    def rows_at(offset):
        return pl.ds(pl.multiple_of(offset, TOK), TOK)

    def home_queries(h):
        for t in range(2):
            for i in range(ROW):
                go_home(og.at[t, h, rows_at(lax.rem(spot + i, ROW) * TOK), :], t, h, i)

    def home_keys(h):
        for t in range(2):
            for i in range(ROW):
                go_home(dkv.at[t, h, rows_at(HALO + lax.rem(spot + i, ROW) * TOK), :], 2 + t, h, i)

    def set_limits():
        all_docs = docs[...]
        own = docs[pl.ds(pl.multiple_of(base * (TOK // HEAD), 16), SPAN // HEAD), :]
        starts = jnp.zeros_like(own)
        for d in range(1, DOCS):
            below_d = jnp.where(all_docs < d, 1.0, 0.0)
            count = jnp.sum(jnp.sum(below_d, axis=0, keepdims=True), axis=1, keepdims=True)
            starts = jnp.where(own == d, jnp.broadcast_to(count.astype(jnp.int32), own.shape), starts)
        limits[...] = starts - (base * TOK - HALO)

    key_iota = lax.broadcasted_iota(jnp.int32, (TOK, TOK), 0)
    diagonal = key_iota <= lax.broadcasted_iota(jnp.int32, (TOK, TOK), 1)
    reach = HALO // TOK + 1

    def prepare(h):
        for b in range(KEYS // TOK):
            span = pl.ds(b * TOK, TOK)
            keys_t[:, span] = kv[0, h, span, :].T
            values_t[:, span] = kv[1, h, span, :].T
        dk_acc[...] = jnp.zeros_like(dk_acc)
        dv_acc[...] = jnp.zeros_like(dv_acc)

    def attend(h, first, last):
        def one_block(b, carry):
            rows = rows_at(b * TOK)
            low = jnp.concatenate([limits[pl.ds(2 * b, 1), :], limits[pl.ds(2 * b + 1, 1), :]], axis=1)
            queries = qg[0, h, rows, :]
            queries_t = queries.T
            cot_raw_t = qg[1, h, rows, :].T

            def key_rows(o):
                return rows_at((b + reach - 1 - o) * TOK)

            peak = jnp.full((1, TOK), NEG, F32)
            for o in range(reach):
                raw = dot(kv[0, h, key_rows(o), :], queries_t)
                inside = key_iota >= low - (b + reach - 1 - o) * TOK
                if o == 0:
                    inside = inside & diagonal
                raw = jnp.where(inside, raw, NEG)
                scores[o] = raw
                peak = jnp.maximum(peak, jnp.max(raw, axis=0, keepdims=True))
            shift = peak * log_scale
            total = jnp.zeros((1, TOK), F32)
            mixed = jnp.zeros((HEAD, TOK), F32)
            for o in range(reach):
                expo = jnp.exp2(scores[o] * log_scale - shift)
                small = expo.astype(BF16)
                weights[o] = small
                total = total + jnp.sum(expo, axis=0, keepdims=True)
                mixed = mixed + dot(values_t[:, key_rows(o)], small)
            inverse = 1.0 / total
            mixed = mixed * inverse
            og[0, h, rows, :] = mixed.T.astype(BF16)
            cot_t = (cot_raw_t.astype(F32) * inverse).astype(BF16)
            rowdot = jnp.sum(cot_t.astype(F32) * mixed, axis=0, keepdims=True)
            cot = cot_t.T
            grad = jnp.zeros((HEAD, TOK), F32)
            for o in range(reach):
                keys = key_rows(o)
                weight = weights[o]
                dweight = dot(kv[1, h, keys, :], cot_t)
                dscore = (weight.astype(F32) * (dweight - rowdot)).astype(BF16)
                dv_acc[keys, :] += dot(weight, cot)
                dk_acc[keys, :] += dot(dscore, queries)
                grad = grad + dot(keys_t[:, keys], dscore)
            og[1, h, rows, :] = (grad * scale).T.astype(BF16)
            return carry

        lax.fori_loop(first, last, one_block, 0)

    def settle(h, first, last):
        for b in range(first, last):
            span = pl.ds(b * TOK, TOK)
            dkv[0, h, span, :] = (dk_acc[span, :] * scale).astype(BF16)
            dkv[1, h, span, :] = dv_acc[span, :].astype(BF16)

    def join(h):
        for t in range(2):
            drop(t, h).wait_recv()
            for b in range(4):
                span = pl.ds(2 * HALO + b * TOK, TOK)
                near = dkv[t, h, span, :].astype(F32)
                dkv[t, h, span, :] = (near + far[t, h, pl.ds(b * TOK, TOK), :].astype(F32)).astype(BF16)
        home_keys(h)

    send(k, 0, 0)
    send(v, 1, 0)
    fetch.wait()
    set_limits()
    raise_half(0, 0)
    send(q, 2, 0)
    raise_half(1, 0)
    send(g, 3, 0)
    send(k, 0, 1)
    send(v, 1, 1)
    send(q, 2, 1)
    send(g, 3, 1)
    arrive(0)
    prepare(0)
    attend(0, 0, 4)
    raise_half(0, 1)
    settle(0, 0, 4)
    for t in range(2):
        drop(t, 0).start()
    attend(0, 4, 8)
    raise_half(1, 1)
    settle(0, 4, 12)
    home_queries(0)
    arrive(1)
    join(0)
    prepare(1)
    attend(1, 0, 4)
    settle(1, 0, 4)
    for t in range(2):
        drop(t, 1).start()
    attend(1, 4, 8)
    settle(1, 4, 12)
    home_queries(1)
    join(1)

    for h in range(2):
        for t in range(2):
            climb(t, h).wait_send()
            drop(t, h).wait_send()
        for t in range(4):
            wait_bytes(qg.at[0, 0, pl.ds(0, (ROW * CHAN - 1) * PIECE), :], send_sem.at[t, h])
            wait_bytes(og.at[0, 0, pl.ds(0, (ROW - 1) * TOK), :], home_send.at[t, h])
            wait_bytes(land.at[t, h], home_recv.at[t, h])


def whole(rows_total, docs, q, k, v, g):
    any_space = pl.BlockSpec(memory_space=pl.ANY)
    vmem = pl.BlockSpec(memory_space=pltpu.VMEM)
    dma = pltpu.SemaphoreType.DMA
    return pl.pallas_call(
        functools.partial(whole_kernel, rows_total),
        out_shape=jax.ShapeDtypeStruct((4, 2, ROW, TOK, HEAD), BF16),
        in_specs=[pl.BlockSpec(memory_space=pltpu.MemorySpace.HBM)] * 5,
        out_specs=pl.BlockSpec(memory_space=pltpu.MemorySpace.VMEM),
        scratch_shapes=[
            pltpu.VMEM((docs.shape[0] // HEAD, HEAD), jnp.int32),
            pltpu.VMEM((2, 2, KEYS, HEAD), BF16),
            pltpu.VMEM((2, 2, SPAN, HEAD), BF16),
            pltpu.VMEM((2, 2, SPAN, HEAD), BF16),
            pltpu.VMEM((2, 2, KEYS, HEAD), BF16),
            pltpu.VMEM((2, 2, HALO, HEAD), BF16),
            pltpu.VMEM((5, TOK, TOK), F32),
            pltpu.VMEM((5, TOK, TOK), BF16),
            pltpu.VMEM((HEAD, KEYS), BF16),
            pltpu.VMEM((HEAD, KEYS), BF16),
            pltpu.VMEM((KEYS, HEAD), F32),
            pltpu.VMEM((KEYS, HEAD), F32),
            pltpu.VMEM((SPAN // HEAD, HEAD), jnp.int32),
            dma((4, 2)),
            dma((4, 2, 2)),
            dma((2, 2)),
            dma((2, 2)),
            dma((2, 2)),
            dma((2, 2)),
            dma((4, 2)),
            dma((4, 2)),
            dma,
        ],
        compiler_params=pltpu.CompilerParams(
            collective_id=0, has_side_effects=True, vmem_limit_bytes=48 << 20
        ),
        name="whole_rows",
    )(*[pltpu.with_memory_space_constraint(a, pltpu.MemorySpace.HBM) for a in (q, k, v, g, docs.reshape(-1, HEAD))])


def lay_kernel(land, o0, o1, o2, o3, out_sem):
    outs = (o0, o1, o2, o3)
    for t in range(4):
        for h in range(2):
            for r in range(ROW):
                lanes = pl.ds((2 * r + h) * HEAD, HEAD)
                pltpu.make_async_copy(land.at[t, h, r], outs[t].at[:, lanes], out_sem.at[t]).start()
    for t in range(4):
        pltpu.make_async_copy(outs[t], outs[t], out_sem.at[t]).wait()


def lay_out(land):
    any_space = pl.BlockSpec(memory_space=pl.ANY)
    land = pltpu.with_memory_space_constraint(land, pltpu.MemorySpace.VMEM)
    return pl.pallas_call(
        lay_kernel,
        out_shape=tuple(jax.ShapeDtypeStruct((TOK, ROW * PAIR), BF16) for _ in range(4)),
        in_specs=[pl.BlockSpec(memory_space=pltpu.MemorySpace.VMEM)],
        out_specs=(any_space,) * 4,
        scratch_shapes=[pltpu.SemaphoreType.DMA((4,))],
        compiler_params=pltpu.CompilerParams(vmem_limit_bytes=8 << 20),
        name="lay_out",
    )(land)


def solution(mesh):
    rows_total = mesh.shape["seq"]

    def on_device(doc_ids, attn_queries, attn_keys, attn_values, attn_cot):
        land = whole(rows_total, doc_ids, attn_queries, attn_keys, attn_values, attn_cot)
        return lay_out(land)

    tokens = P(("seq", "chan"), None)
    return jax.shard_map(
        on_device,
        mesh=mesh,
        in_specs=(P(), tokens, tokens, tokens, tokens),
        out_specs=(P("seq", "chan"),) * 4,
        check_vma=False,
    )
```

```python
import functools

import jax
import jax.numpy as jnp
from jax import lax
from jax.experimental import pallas as pl
from jax.experimental.pallas import tpu as pltpu
from jax.sharding import PartitionSpec as P

MESH = pl.DeviceIdType.MESH
HEAD = 128
ROW = 8
CHAN = 4
TOK = 256
PIECE = 64
SPAN = ROW * TOK
HALO = 1024
KEYS = SPAN + HALO
PAIR = 2 * HEAD
LOG2E = 1.4426950408889634
NEG = -1e30
F32 = jnp.float32
BF16 = jnp.bfloat16
DOCS = 16


def place():
    shard = lax.axis_index("seq")
    plane = lax.axis_index("chan")
    spot = lax.rem(shard, ROW)
    return shard - spot, spot, plane


def wait_bytes(ref, sem):
    pltpu.make_async_copy(ref, ref, sem).wait()


def dot(a, b):
    return jnp.dot(a, b, preferred_element_type=F32)


def whole_kernel(
    rows_total, q, k, v, g, docs_far, land,
    docs, kv, qg, og, dkv, far, scores, weights, keys_t, values_t, dk_acc, dv_acc, limits,
    send_sem, recv_sem, up_send, up_recv, down_send, down_recv, home_send, home_recv, docs_sem,
):
    base, spot, plane = place()
    half = spot // 4
    above = (lax.rem(base + ROW, rows_total) + spot, plane)
    below = (lax.rem(base + rows_total - ROW, rows_total) + spot, plane)
    scale = HEAD ** -0.5
    log_scale = scale * LOG2E

    fetch = pltpu.make_async_copy(docs_far, docs, docs_sem)
    fetch.start()
    bar = pltpu.get_barrier_semaphore()
    pl.semaphore_signal(bar, inc=1, device_id=above, device_id_type=MESH)
    pl.semaphore_signal(bar, inc=1, device_id=below, device_id_type=MESH)
    order = [(i, j) for j in (2, 1, 3, 0) for i in (4, 5, 2, 3, 6, 7, 1, 0) if i or j]
    for i, j in order:
        peer = (base + lax.rem(spot + i, ROW), lax.rem(plane + j, CHAN))
        pl.semaphore_signal(bar, inc=1, device_id=peer, device_id_type=MESH)
    pl.semaphore_wait(bar, ROW * CHAN + 1)

    def send(src, t, h):
        offset = spot * TOK + plane * PIECE + (HALO if t < 2 else 0)
        rows = pl.ds(pl.multiple_of(offset, PIECE), PIECE)
        dst = (kv if t < 2 else qg).at[t % 2, h, rows, :]
        arrival = recv_sem.at[t, h, half]

        def columns(room, floor):
            first = (floor * ROW + room) * PAIR + h * HEAD
            return pl.ds(pl.multiple_of(first, HEAD), HEAD)

        pltpu.make_async_copy(src.at[:, columns(spot, plane)], dst, arrival).start()

        def one(n, carry):
            room = lax.rem(spot + 3 * lax.rem(n, ROW) + n // ROW, ROW)
            floor = lax.rem(plane + lax.rem(n, CHAN), CHAN)
            pltpu.make_async_remote_copy(
                src_ref=src.at[:, columns(room, floor)],
                dst_ref=dst,
                send_sem=send_sem.at[t, h],
                recv_sem=arrival,
                device_id=(base + room, floor),
                device_id_type=MESH,
            ).start()
            return carry

        lax.fori_loop(1, ROW * CHAN, one, 0)

    def climb(t, h):
        return pltpu.make_async_remote_copy(
            src_ref=kv.at[t, h, pl.ds(2 * HALO, HALO), :],
            dst_ref=kv.at[t, h, pl.ds(0, HALO), :],
            send_sem=up_send.at[t, h],
            recv_sem=up_recv.at[t, h],
            device_id=above,
            device_id_type=MESH,
        )

    def raise_half(t, h):
        wait_bytes(kv.at[t, h, pl.ds(2 * HALO, HALO), :], recv_sem.at[t, h, 1])
        climb(t, h).start()

    def arrive(h):
        for t in range(2):
            wait_bytes(kv.at[t, h, pl.ds(HALO, HALO), :], recv_sem.at[t, h, 0])
            wait_bytes(qg.at[t, h, pl.ds(0, HALO), :], recv_sem.at[2 + t, h, 0])
            wait_bytes(qg.at[t, h, pl.ds(HALO, HALO), :], recv_sem.at[2 + t, h, 1])
        for t in range(2):
            climb(t, h).wait_recv()

    def drop(t, h):
        return pltpu.make_async_remote_copy(
            src_ref=dkv.at[t, h, pl.ds(0, HALO), :],
            dst_ref=far.at[t, h],
            send_sem=down_send.at[t, h],
            recv_sem=down_recv.at[t, h],
            device_id=below,
            device_id_type=MESH,
        )

    def go_home(src, t, h, i):
        other = lax.rem(spot + i, ROW)
        dst = land.at[t, h, spot]
        if i == 0:
            pltpu.make_async_copy(src, dst, home_recv.at[t, h]).start()
        else:
            pltpu.make_async_remote_copy(
                src_ref=src,
                dst_ref=dst,
                send_sem=home_send.at[t, h],
                recv_sem=home_recv.at[t, h],
                device_id=(base + other, plane),
                device_id_type=MESH,
            ).start()

    def rows_at(offset):
        return pl.ds(pl.multiple_of(offset, TOK), TOK)

    def home_queries(h):
        for t in range(2):
            for i in range(ROW):
                go_home(og.at[t, h, rows_at(lax.rem(spot + i, ROW) * TOK), :], t, h, i)

    def home_keys(h):
        for t in range(2):
            for i in range(ROW):
                go_home(dkv.at[t, h, rows_at(HALO + lax.rem(spot + i, ROW) * TOK), :], 2 + t, h, i)

    def set_limits():
        all_docs = docs[...]
        own = docs[pl.ds(pl.multiple_of(base * (TOK // HEAD), 16), SPAN // HEAD), :]
        starts = jnp.zeros_like(own)
        for d in range(1, DOCS):
            below_d = jnp.where(all_docs < d, 1.0, 0.0)
            count = jnp.sum(jnp.sum(below_d, axis=0, keepdims=True), axis=1, keepdims=True)
            starts = jnp.where(own == d, jnp.broadcast_to(count.astype(jnp.int32), own.shape), starts)
        limits[...] = starts - (base * TOK - HALO)

    key_iota = lax.broadcasted_iota(jnp.int32, (TOK, TOK), 0)
    diagonal = key_iota <= lax.broadcasted_iota(jnp.int32, (TOK, TOK), 1)
    reach = HALO // TOK + 1

    def prepare(h):
        for b in range(KEYS // TOK):
            span = pl.ds(b * TOK, TOK)
            keys_t[:, span] = kv[0, h, span, :].T
            values_t[:, span] = kv[1, h, span, :].T
        dk_acc[...] = jnp.zeros_like(dk_acc)
        dv_acc[...] = jnp.zeros_like(dv_acc)

    def attend(h, first, last):
        def one_block(b, carry):
            rows = rows_at(b * TOK)
            low = jnp.concatenate([limits[pl.ds(2 * b, 1), :], limits[pl.ds(2 * b + 1, 1), :]], axis=1)
            queries = qg[0, h, rows, :]
            queries_t = queries.T
            cot_raw_t = qg[1, h, rows, :].T

            def key_rows(o):
                return rows_at((b + reach - 1 - o) * TOK)

            peak = jnp.full((1, TOK), NEG, F32)
            for o in range(reach):
                raw = dot(kv[0, h, key_rows(o), :], queries_t)
                inside = key_iota >= low - (b + reach - 1 - o) * TOK
                if o == 0:
                    inside = inside & diagonal
                raw = jnp.where(inside, raw, NEG)
                scores[o] = raw
                peak = jnp.maximum(peak, jnp.max(raw, axis=0, keepdims=True))
            shift = peak * log_scale
            total = jnp.zeros((1, TOK), F32)
            mixed = jnp.zeros((HEAD, TOK), F32)
            for o in range(reach):
                expo = jnp.exp2(scores[o] * log_scale - shift)
                small = expo.astype(BF16)
                weights[o] = small
                total = total + jnp.sum(expo, axis=0, keepdims=True)
                mixed = mixed + dot(values_t[:, key_rows(o)], small)
            inverse = 1.0 / total
            mixed = mixed * inverse
            og[0, h, rows, :] = mixed.T.astype(BF16)
            cot_t = (cot_raw_t.astype(F32) * inverse).astype(BF16)
            rowdot = jnp.sum(cot_t.astype(F32) * mixed, axis=0, keepdims=True)
            cot = cot_t.T
            grad = jnp.zeros((HEAD, TOK), F32)
            for o in range(reach):
                keys = key_rows(o)
                weight = weights[o]
                dweight = dot(kv[1, h, keys, :], cot_t)
                dscore = (weight.astype(F32) * (dweight - rowdot)).astype(BF16)
                dv_acc[keys, :] += dot(weight, cot)
                dk_acc[keys, :] += dot(dscore, queries)
                grad = grad + dot(keys_t[:, keys], dscore)
            og[1, h, rows, :] = (grad * scale).T.astype(BF16)
            return carry

        lax.fori_loop(first, last, one_block, 0)

    def settle(h, first, last):
        for b in range(first, last):
            span = pl.ds(b * TOK, TOK)
            dkv[0, h, span, :] = (dk_acc[span, :] * scale).astype(BF16)
            dkv[1, h, span, :] = dv_acc[span, :].astype(BF16)

    def join(h):
        for t in range(2):
            drop(t, h).wait_recv()
            for b in range(4):
                span = pl.ds(2 * HALO + b * TOK, TOK)
                near = dkv[t, h, span, :].astype(F32)
                dkv[t, h, span, :] = (near + far[t, h, pl.ds(b * TOK, TOK), :].astype(F32)).astype(BF16)
        home_keys(h)

    send(k, 0, 0)
    send(v, 1, 0)
    fetch.wait()
    set_limits()
    raise_half(0, 0)
    send(q, 2, 0)
    raise_half(1, 0)
    send(g, 3, 0)
    send(k, 0, 1)
    send(v, 1, 1)
    send(q, 2, 1)
    send(g, 3, 1)
    arrive(0)
    prepare(0)
    attend(0, 0, 4)
    raise_half(0, 1)
    settle(0, 0, 4)
    for t in range(2):
        drop(t, 0).start()
    attend(0, 4, 8)
    raise_half(1, 1)
    settle(0, 4, 12)
    home_queries(0)
    arrive(1)
    join(0)
    prepare(1)
    attend(1, 0, 4)
    settle(1, 0, 4)
    for t in range(2):
        drop(t, 1).start()
    attend(1, 4, 8)
    settle(1, 4, 12)
    home_queries(1)
    join(1)

    for h in range(2):
        for t in range(2):
            climb(t, h).wait_send()
            drop(t, h).wait_send()
        for t in range(4):
            wait_bytes(qg.at[0, 0, pl.ds(0, (ROW * CHAN - 1) * PIECE), :], send_sem.at[t, h])
            wait_bytes(og.at[0, 0, pl.ds(0, (ROW - 1) * TOK), :], home_send.at[t, h])
            wait_bytes(land.at[t, h], home_recv.at[t, h])


def whole(rows_total, docs, q, k, v, g):
    any_space = pl.BlockSpec(memory_space=pl.ANY)
    vmem = pl.BlockSpec(memory_space=pltpu.VMEM)
    dma = pltpu.SemaphoreType.DMA
    return pl.pallas_call(
        functools.partial(whole_kernel, rows_total),
        out_shape=jax.ShapeDtypeStruct((4, 2, ROW, TOK, HEAD), BF16),
        in_specs=[pl.BlockSpec(memory_space=pltpu.MemorySpace.HBM)] * 5,
        out_specs=pl.BlockSpec(memory_space=pltpu.MemorySpace.VMEM),
        scratch_shapes=[
            pltpu.VMEM((docs.shape[0] // HEAD, HEAD), jnp.int32),
            pltpu.VMEM((2, 2, KEYS, HEAD), BF16),
            pltpu.VMEM((2, 2, SPAN, HEAD), BF16),
            pltpu.VMEM((2, 2, SPAN, HEAD), BF16),
            pltpu.VMEM((2, 2, KEYS, HEAD), BF16),
            pltpu.VMEM((2, 2, HALO, HEAD), BF16),
            pltpu.VMEM((5, TOK, TOK), F32),
            pltpu.VMEM((5, TOK, TOK), BF16),
            pltpu.VMEM((HEAD, KEYS), BF16),
            pltpu.VMEM((HEAD, KEYS), BF16),
            pltpu.VMEM((KEYS, HEAD), F32),
            pltpu.VMEM((KEYS, HEAD), F32),
            pltpu.VMEM((SPAN // HEAD, HEAD), jnp.int32),
            dma((4, 2)),
            dma((4, 2, 2)),
            dma((2, 2)),
            dma((2, 2)),
            dma((2, 2)),
            dma((2, 2)),
            dma((4, 2)),
            dma((4, 2)),
            dma,
        ],
        compiler_params=pltpu.CompilerParams(
            collective_id=0, has_side_effects=True, vmem_limit_bytes=48 << 20
        ),
        name="whole_rows",
    )(*[pltpu.with_memory_space_constraint(a, pltpu.MemorySpace.HBM) for a in (q, k, v, g, docs.reshape(-1, HEAD))])


def lay_kernel(land, o0, o1, o2, o3, out_sem):
    outs = (o0, o1, o2, o3)
    for t in range(4):
        for h in range(2):
            for r in range(ROW):
                lanes = pl.ds((2 * r + h) * HEAD, HEAD)
                pltpu.make_async_copy(land.at[t, h, r], outs[t].at[:, lanes], out_sem.at[t]).start()
    for t in range(4):
        pltpu.make_async_copy(outs[t], outs[t], out_sem.at[t]).wait()


def lay_out(land):
    any_space = pl.BlockSpec(memory_space=pl.ANY)
    land = pltpu.with_memory_space_constraint(land, pltpu.MemorySpace.VMEM)
    return pl.pallas_call(
        lay_kernel,
        out_shape=tuple(jax.ShapeDtypeStruct((TOK, ROW * PAIR), BF16) for _ in range(4)),
        in_specs=[pl.BlockSpec(memory_space=pltpu.MemorySpace.VMEM)],
        out_specs=(any_space,) * 4,
        scratch_shapes=[pltpu.SemaphoreType.DMA((4,))],
        compiler_params=pltpu.CompilerParams(vmem_limit_bytes=8 << 20),
        name="lay_out",
    )(land)


def solution(mesh):
    rows_total = mesh.shape["seq"]

    def on_device(doc_ids, attn_queries, attn_keys, attn_values, attn_cot):
        land = whole(rows_total, doc_ids, attn_queries, attn_keys, attn_values, attn_cot)
        return lay_out(land)

    tokens = P(("seq", "chan"), None)
    return jax.shard_map(
        on_device,
        mesh=mesh,
        in_specs=(P(), tokens, tokens, tokens, tokens),
        out_specs=(P("seq", "chan"),) * 4,
        check_vma=False,
    )
```

```python
import functools

import jax
import jax.numpy as jnp
from jax import lax
from jax.experimental import pallas as pl
from jax.experimental.pallas import tpu as pltpu
from jax.sharding import PartitionSpec as P

MESH = pl.DeviceIdType.MESH
HEAD = 128
ROW = 8
CHAN = 4
TOK = 256
PIECE = 64
SPAN = ROW * TOK
HALO = 1024
KEYS = SPAN + HALO
PAIR = 2 * HEAD
LOG2E = 1.4426950408889634
NEG = -1e30
F32 = jnp.float32
BF16 = jnp.bfloat16
DOCS = 16


def place():
    shard = lax.axis_index("seq")
    plane = lax.axis_index("chan")
    spot = lax.rem(shard, ROW)
    return shard - spot, spot, plane


def wait_bytes(ref, sem):
    pltpu.make_async_copy(ref, ref, sem).wait()


def dot(a, b):
    return jnp.dot(a, b, preferred_element_type=F32)


def whole_kernel(
    rows_total, q, k, v, g, docs_far, land,
    docs, kv, qg, og, dkv, far, scores, weights, keys_t, values_t, dk_acc, dv_acc, limits,
    send_sem, recv_sem, up_send, up_recv, down_send, down_recv, home_send, home_recv, docs_sem,
):
    base, spot, plane = place()
    half = spot // 4
    above = (lax.rem(base + ROW, rows_total) + spot, plane)
    below = (lax.rem(base + rows_total - ROW, rows_total) + spot, plane)
    scale = HEAD ** -0.5
    log_scale = scale * LOG2E

    fetch = pltpu.make_async_copy(docs_far, docs, docs_sem)
    fetch.start()
    bar = pltpu.get_barrier_semaphore()
    pl.semaphore_signal(bar, inc=1, device_id=above, device_id_type=MESH)
    pl.semaphore_signal(bar, inc=1, device_id=below, device_id_type=MESH)
    order = [(i, j) for j in (2, 1, 3, 0) for i in (4, 5, 2, 3, 6, 7, 1, 0) if i or j]
    for i, j in order:
        peer = (base + lax.rem(spot + i, ROW), lax.rem(plane + j, CHAN))
        pl.semaphore_signal(bar, inc=1, device_id=peer, device_id_type=MESH)
    pl.semaphore_wait(bar, ROW * CHAN + 1)

    def send(src, t, h):
        offset = spot * TOK + plane * PIECE + (HALO if t < 2 else 0)
        rows = pl.ds(pl.multiple_of(offset, PIECE), PIECE)
        dst = (kv if t < 2 else qg).at[t % 2, h, rows, :]
        arrival = recv_sem.at[t, h, half]

        def columns(room, floor):
            first = (floor * ROW + room) * PAIR + h * HEAD
            return pl.ds(pl.multiple_of(first, HEAD), HEAD)

        pltpu.make_async_copy(src.at[:, columns(spot, plane)], dst, arrival).start()

        def one(n, carry):
            room = lax.rem(spot + 3 * lax.rem(n, ROW) + n // ROW, ROW)
            floor = lax.rem(plane + lax.rem(n, CHAN), CHAN)
            pltpu.make_async_remote_copy(
                src_ref=src.at[:, columns(room, floor)],
                dst_ref=dst,
                send_sem=send_sem.at[t, h],
                recv_sem=arrival,
                device_id=(base + room, floor),
                device_id_type=MESH,
            ).start()
            return carry

        lax.fori_loop(1, ROW * CHAN, one, 0)

    def climb(t, h):
        return pltpu.make_async_remote_copy(
            src_ref=kv.at[t, h, pl.ds(2 * HALO, HALO), :],
            dst_ref=kv.at[t, h, pl.ds(0, HALO), :],
            send_sem=up_send.at[t, h],
            recv_sem=up_recv.at[t, h],
            device_id=above,
            device_id_type=MESH,
        )

    def raise_half(t, h):
        wait_bytes(kv.at[t, h, pl.ds(2 * HALO, HALO), :], recv_sem.at[t, h, 1])
        climb(t, h).start()

    def arrive(h):
        for t in range(2):
            wait_bytes(kv.at[t, h, pl.ds(HALO, HALO), :], recv_sem.at[t, h, 0])
            wait_bytes(qg.at[t, h, pl.ds(0, HALO), :], recv_sem.at[2 + t, h, 0])
            wait_bytes(qg.at[t, h, pl.ds(HALO, HALO), :], recv_sem.at[2 + t, h, 1])
        for t in range(2):
            climb(t, h).wait_recv()

    def drop(t, h):
        return pltpu.make_async_remote_copy(
            src_ref=dkv.at[t, h, pl.ds(0, HALO), :],
            dst_ref=far.at[t, h],
            send_sem=down_send.at[t, h],
            recv_sem=down_recv.at[t, h],
            device_id=below,
            device_id_type=MESH,
        )

    def go_home(src, t, h, i):
        other = lax.rem(spot + i, ROW)
        dst = land.at[t, h, spot]
        if i == 0:
            pltpu.make_async_copy(src, dst, home_recv.at[t, h]).start()
        else:
            pltpu.make_async_remote_copy(
                src_ref=src,
                dst_ref=dst,
                send_sem=home_send.at[t, h],
                recv_sem=home_recv.at[t, h],
                device_id=(base + other, plane),
                device_id_type=MESH,
            ).start()

    def rows_at(offset):
        return pl.ds(pl.multiple_of(offset, TOK), TOK)

    def home_queries(h, upper):
        for t in range(2):
            for i in range(ROW):
                other = lax.rem(spot + i, ROW)

                @pl.when((other >= 4) if upper else (other < 4))
                def _():
                    go_home(og.at[t, h, rows_at(other * TOK), :], t, h, i)

    def home_keys(h):
        for t in range(2):
            for i in range(ROW):
                go_home(dkv.at[t, h, rows_at(HALO + lax.rem(spot + i, ROW) * TOK), :], 2 + t, h, i)

    def set_limits():
        all_docs = docs[...]
        own = docs[pl.ds(pl.multiple_of(base * (TOK // HEAD), 16), SPAN // HEAD), :]
        starts = jnp.zeros_like(own)
        for d in range(1, DOCS):
            below_d = jnp.where(all_docs < d, 1.0, 0.0)
            count = jnp.sum(jnp.sum(below_d, axis=0, keepdims=True), axis=1, keepdims=True)
            starts = jnp.where(own == d, jnp.broadcast_to(count.astype(jnp.int32), own.shape), starts)
        limits[...] = starts - (base * TOK - HALO)

    key_iota = lax.broadcasted_iota(jnp.int32, (TOK, TOK), 0)
    diagonal = key_iota <= lax.broadcasted_iota(jnp.int32, (TOK, TOK), 1)
    reach = HALO // TOK + 1

    def prepare(h):
        for b in range(KEYS // TOK):
            span = pl.ds(b * TOK, TOK)
            keys_t[:, span] = kv[0, h, span, :].T
            values_t[:, span] = kv[1, h, span, :].T
        dk_acc[...] = jnp.zeros_like(dk_acc)
        dv_acc[...] = jnp.zeros_like(dv_acc)

    def attend(h, first, last):
        def one_block(b, carry):
            rows = rows_at(b * TOK)
            low = jnp.concatenate([limits[pl.ds(2 * b, 1), :], limits[pl.ds(2 * b + 1, 1), :]], axis=1)
            queries = qg[0, h, rows, :]
            queries_t = queries.T
            cot_raw_t = qg[1, h, rows, :].T

            def key_rows(o):
                return rows_at((b + reach - 1 - o) * TOK)

            peak = jnp.full((1, TOK), NEG, F32)
            for o in range(reach):
                raw = dot(kv[0, h, key_rows(o), :], queries_t)
                inside = key_iota >= low - (b + reach - 1 - o) * TOK
                if o == 0:
                    inside = inside & diagonal
                raw = jnp.where(inside, raw, NEG)
                scores[o] = raw
                peak = jnp.maximum(peak, jnp.max(raw, axis=0, keepdims=True))
            shift = peak * log_scale
            total = jnp.zeros((1, TOK), F32)
            mixed = jnp.zeros((HEAD, TOK), F32)
            for o in range(reach):
                expo = jnp.exp2(scores[o] * log_scale - shift)
                small = expo.astype(BF16)
                weights[o] = small
                total = total + jnp.sum(expo, axis=0, keepdims=True)
                mixed = mixed + dot(values_t[:, key_rows(o)], small)
            inverse = 1.0 / total
            mixed = mixed * inverse
            og[0, h, rows, :] = mixed.T.astype(BF16)
            cot_t = (cot_raw_t.astype(F32) * inverse).astype(BF16)
            rowdot = jnp.sum(cot_t.astype(F32) * mixed, axis=0, keepdims=True)
            cot = cot_t.T
            grad = jnp.zeros((HEAD, TOK), F32)
            for o in range(reach):
                keys = key_rows(o)
                weight = weights[o]
                dweight = dot(kv[1, h, keys, :], cot_t)
                dscore = (weight.astype(F32) * (dweight - rowdot)).astype(BF16)
                dv_acc[keys, :] += dot(weight, cot)
                dk_acc[keys, :] += dot(dscore, queries)
                grad = grad + dot(keys_t[:, keys], dscore)
            og[1, h, rows, :] = (grad * scale).T.astype(BF16)
            return carry

        lax.fori_loop(first, last, one_block, 0)

    def settle(h, first, last):
        for b in range(first, last):
            span = pl.ds(b * TOK, TOK)
            dkv[0, h, span, :] = (dk_acc[span, :] * scale).astype(BF16)
            dkv[1, h, span, :] = dv_acc[span, :].astype(BF16)

    def join(h):
        for t in range(2):
            drop(t, h).wait_recv()
            for b in range(4):
                span = pl.ds(2 * HALO + b * TOK, TOK)
                near = dkv[t, h, span, :].astype(F32)
                dkv[t, h, span, :] = (near + far[t, h, pl.ds(b * TOK, TOK), :].astype(F32)).astype(BF16)
        home_keys(h)

    send(k, 0, 0)
    send(v, 1, 0)
    fetch.wait()
    set_limits()
    raise_half(0, 0)
    send(q, 2, 0)
    raise_half(1, 0)
    send(g, 3, 0)
    send(k, 0, 1)
    send(v, 1, 1)
    send(q, 2, 1)
    send(g, 3, 1)
    arrive(0)
    prepare(0)
    attend(0, 0, 4)
    raise_half(0, 1)
    settle(0, 0, 4)
    for t in range(2):
        drop(t, 0).start()
    home_queries(0, False)
    attend(0, 4, 8)
    raise_half(1, 1)
    settle(0, 4, 12)
    home_queries(0, True)
    arrive(1)
    join(0)
    prepare(1)
    attend(1, 0, 4)
    settle(1, 0, 4)
    for t in range(2):
        drop(t, 1).start()
    home_queries(1, False)
    attend(1, 4, 8)
    settle(1, 4, 12)
    home_queries(1, True)
    join(1)

    for h in range(2):
        for t in range(2):
            climb(t, h).wait_send()
            drop(t, h).wait_send()
        for t in range(4):
            wait_bytes(qg.at[0, 0, pl.ds(0, (ROW * CHAN - 1) * PIECE), :], send_sem.at[t, h])
            wait_bytes(og.at[0, 0, pl.ds(0, (ROW - 1) * TOK), :], home_send.at[t, h])
            wait_bytes(land.at[t, h], home_recv.at[t, h])


def whole(rows_total, docs, q, k, v, g):
    any_space = pl.BlockSpec(memory_space=pl.ANY)
    vmem = pl.BlockSpec(memory_space=pltpu.VMEM)
    dma = pltpu.SemaphoreType.DMA
    return pl.pallas_call(
        functools.partial(whole_kernel, rows_total),
        out_shape=jax.ShapeDtypeStruct((4, 2, ROW, TOK, HEAD), BF16),
        in_specs=[pl.BlockSpec(memory_space=pltpu.MemorySpace.HBM)] * 5,
        out_specs=pl.BlockSpec(memory_space=pltpu.MemorySpace.VMEM),
        scratch_shapes=[
            pltpu.VMEM((docs.shape[0] // HEAD, HEAD), jnp.int32),
            pltpu.VMEM((2, 2, KEYS, HEAD), BF16),
            pltpu.VMEM((2, 2, SPAN, HEAD), BF16),
            pltpu.VMEM((2, 2, SPAN, HEAD), BF16),
            pltpu.VMEM((2, 2, KEYS, HEAD), BF16),
            pltpu.VMEM((2, 2, HALO, HEAD), BF16),
            pltpu.VMEM((5, TOK, TOK), F32),
            pltpu.VMEM((5, TOK, TOK), BF16),
            pltpu.VMEM((HEAD, KEYS), BF16),
            pltpu.VMEM((HEAD, KEYS), BF16),
            pltpu.VMEM((KEYS, HEAD), F32),
            pltpu.VMEM((KEYS, HEAD), F32),
            pltpu.VMEM((SPAN // HEAD, HEAD), jnp.int32),
            dma((4, 2)),
            dma((4, 2, 2)),
            dma((2, 2)),
            dma((2, 2)),
            dma((2, 2)),
            dma((2, 2)),
            dma((4, 2)),
            dma((4, 2)),
            dma,
        ],
        compiler_params=pltpu.CompilerParams(
            collective_id=0, has_side_effects=True, vmem_limit_bytes=48 << 20
        ),
        name="whole_rows",
    )(*[pltpu.with_memory_space_constraint(a, pltpu.MemorySpace.HBM) for a in (q, k, v, g, docs.reshape(-1, HEAD))])


def lay_kernel(land, o0, o1, o2, o3, out_sem):
    outs = (o0, o1, o2, o3)
    for t in range(4):
        for h in range(2):
            for r in range(ROW):
                lanes = pl.ds((2 * r + h) * HEAD, HEAD)
                pltpu.make_async_copy(land.at[t, h, r], outs[t].at[:, lanes], out_sem.at[t]).start()
    for t in range(4):
        pltpu.make_async_copy(outs[t], outs[t], out_sem.at[t]).wait()


def lay_out(land):
    any_space = pl.BlockSpec(memory_space=pl.ANY)
    land = pltpu.with_memory_space_constraint(land, pltpu.MemorySpace.VMEM)
    return pl.pallas_call(
        lay_kernel,
        out_shape=tuple(jax.ShapeDtypeStruct((TOK, ROW * PAIR), BF16) for _ in range(4)),
        in_specs=[pl.BlockSpec(memory_space=pltpu.MemorySpace.VMEM)],
        out_specs=(any_space,) * 4,
        scratch_shapes=[pltpu.SemaphoreType.DMA((4,))],
        compiler_params=pltpu.CompilerParams(vmem_limit_bytes=8 << 20),
        name="lay_out",
    )(land)


def solution(mesh):
    rows_total = mesh.shape["seq"]

    def on_device(doc_ids, attn_queries, attn_keys, attn_values, attn_cot):
        land = whole(rows_total, doc_ids, attn_queries, attn_keys, attn_values, attn_cot)
        return lay_out(land)

    tokens = P(("seq", "chan"), None)
    return jax.shard_map(
        on_device,
        mesh=mesh,
        in_specs=(P(), tokens, tokens, tokens, tokens),
        out_specs=(P("seq", "chan"),) * 4,
        check_vma=False,
    )
```
